32 devices in a mesh: row: 8 (over z, x), col: 4 (over y, core).
Axes of the slice: x: 2, y: 2, z: 4, core: 2. Of those that a mesh axis runs over, the one named last changes fastest.
Arguments:
- pivot_rows: float32 [3, 512, 6144], P(None, 'row', 'col'), may hold values from 0 to 32002, as said below
- coupling: float32 [3, 512, 512], P(None, 'row', 'col'), may hold values from 0 to 32002, as said below
- inverse: float32 [3, 512, 512], P(None, 'row', 'col'), may hold values from 0 to 32002, as said below
- multipliers: float32 [3, 2048, 512], P(None, 'row', 'col'), may hold values from 0 to 32002, as said below
- tile_mask: int32 [3, 32], P(None, 'row'), may hold values from 0 to 1, as said below
- nonpivot_rows: float32 [2048, 6144], P('row', 'col'), may hold values from 0 to 32002, as said below
Outputs:
- reduced_pivots: float32 [3, 512, 6144], P(None, 'row', 'col')
- reduced_rest: float32 [2048, 6144], P('row', 'col')
The draws below stay inside these ranges and needn't reach their ends.
Inputs may be any that keep to these rules, and one draw needn't show every extreme that they name: `pivot_rows`: whole numbers. `coupling`: whole numbers. `inverse`: whole numbers; each block is unit upper triangular, ones on its diagonal and zeros below it. `multipliers`: whole numbers. `tile_mask`: tile t covers rows t * 64 to (t + 1) * 64 - 1. `nonpivot_rows`: whole numbers.
All inputs are finite; a program needn't handle non-finite values.
Results may differ from the reference program's by a relative error of at most 0.0003.
Values sent between devices are 32-bit elements; how exact they have to be, the bound alone decides.
No kernel may reach another device: no remote copies, remote signals or barrier semaphores. Data moves between devices by JAX's collectives and lax.ppermute only.
A program may use at most 128 MiB of HBM per device.

```python
import jax
import jax.numpy as jnp

PB = 512
TR = 64
ROWS_DEV = 256
NPR = 2048
NCOL = 6144
N_ROW = 8


modulus_int = 32003


def draw_residues(key, shape):
    values = jax.random.randint(key, shape, 0, modulus_int)
    return values.astype(jnp.float32)


def draw_pivot_rows(key, part):
    return draw_residues(key, (3, PB, NCOL))


def draw_coupling(key, part):
    return draw_residues(key, (3, PB, PB))


def draw_inverse(key, part):
    values = draw_residues(key, (3, PB, PB))
    places = jnp.arange(PB)
    above = places[:, None] < places[None, :]
    diagonal = places[:, None] == places[None, :]
    return jnp.where(above[None], values, jnp.where(diagonal[None], 1.0, 0.0)).astype(jnp.float32)


def draw_multipliers(key, part):
    return draw_residues(key, (3, NPR, PB))


def draw_nonpivot_rows(key, part):
    return draw_residues(key, (NPR, NCOL))


def draw_tile_mask(key, part):
    tile_count = NPR // TR
    group = jnp.arange(tile_count) // (ROWS_DEV // TR)
    threshold = 200 + 600 * group // max(N_ROW - 1, 1)
    drawn = jax.random.randint(key, (3, tile_count), 0, 1000)
    return (drawn < threshold[None, :]).astype(jnp.int32)


def setup_inputs(seed: int = 0) -> dict:
    key_list = jax.random.split(jax.random.key(seed), 7)
    return {
        "pivot_rows": draw_pivot_rows(jax.random.fold_in(key_list[6], 71), 0),
        "coupling": draw_coupling(jax.random.fold_in(key_list[6], 71), 0),
        "inverse": draw_inverse(jax.random.fold_in(key_list[6], 71), 0),
        "multipliers": draw_multipliers(jax.random.fold_in(key_list[6], 71), 0),
        "tile_mask": draw_tile_mask(jax.random.fold_in(key_list[6], 71), 0),
        "nonpivot_rows": draw_nonpivot_rows(jax.random.fold_in(key_list[6], 71), 0),
    }


modulus = 32003.0


def reduce_mod(values):
    quotient = jnp.floor(values / modulus)
    rest = values - quotient * modulus
    rest = jnp.where(rest < 0, rest + modulus, rest)
    return jnp.where(rest >= modulus, rest - modulus, rest)


def split_limbs(values):
    upper = jnp.floor(values / 256.0)
    lower = values - upper * 256.0
    return upper.astype(jnp.bfloat16), lower.astype(jnp.bfloat16)


def dotted(first, second):
    return jnp.dot(first, second, preferred_element_type=jnp.float32)


def limb_product(left_pair, right_pair):
    high_high = reduce_mod(dotted(left_pair[0], right_pair[0]))
    middle = reduce_mod(reduce_mod(dotted(left_pair[0], right_pair[1])) + reduce_mod(dotted(left_pair[1], right_pair[0])))
    low_low = reduce_mod(dotted(left_pair[1], right_pair[1]))
    summed = reduce_mod(high_high * 256.0 + middle)
    return reduce_mod(summed * 256.0 + low_low)


def product_mod(left_pair, right_pair):
    inner = left_pair[0].shape[1]
    summed = None
    for first_col in range(0, inner, 256):
        last_col = min(first_col + 256, inner)
        portion = limb_product((left_pair[0][:, first_col:last_col], left_pair[1][:, first_col:last_col]), (right_pair[0][first_col:last_col], right_pair[1][first_col:last_col]))
        summed = portion if summed is None else reduce_mod(summed + portion)
    return summed


def reference(pivot_rows, coupling, inverse, multipliers, tile_mask, nonpivot_rows):
    pair_slot = {(0, 1): 0, (0, 2): 1, (1, 2): 2}
    reduced = [None, None, None]
    for block_index in (2, 1, 0):
        pending = pivot_rows[block_index]
        later_sum = None
        for later_index in range(block_index + 1, 3):
            portion = product_mod(split_limbs(coupling[pair_slot[(block_index, later_index)]]), split_limbs(reduced[later_index]))
            later_sum = portion if later_sum is None else reduce_mod(later_sum + portion)
        if later_sum is not None:
            pending = reduce_mod(pending - later_sum + modulus)
        reduced[block_index] = product_mod(split_limbs(inverse[block_index]), split_limbs(pending))
    tile_count = tile_mask.shape[1]
    row_listed = jnp.broadcast_to(tile_mask[:, :, None], (3, tile_count, TR)).reshape(3, tile_count * TR).astype(jnp.float32)
    listed = multipliers * row_listed[:, :, None]
    update = None
    for block_index in range(3):
        portion = product_mod(split_limbs(listed[block_index]), split_limbs(reduced[block_index]))
        update = portion if update is None else reduce_mod(update + portion)
    residue = reduce_mod(nonpivot_rows - update + modulus)
    return jnp.stack(reduced) / modulus, residue / modulus
```

```python
import functools

import jax
import jax.numpy as jnp
from jax import lax
from jax.experimental import pallas as pl
from jax.experimental.pallas import tpu as pltpu
from jax.sharding import PartitionSpec as P

MODULUS = 32003.0
INVERSE_MODULUS = 1.0 / 32003.0
HALF = 16001.0
BASE = 180.0
INVERSE_BASE = 1.0 / 180.0
SQUARE = float((180 * 180) % 32003)
BLOCKS = 3
LANES = 128


def balanced(values):
    return values - jnp.round(values * INVERSE_MODULUS) * MODULUS


def centred(values):
    return jnp.where(values > HALF, values - MODULUS, values)


def digits(values):
    upper = jnp.round(values * INVERSE_BASE)
    lower = values - upper * BASE
    total = upper + lower
    return (
        upper.astype(jnp.bfloat16),
        lower.astype(jnp.bfloat16),
        total.astype(jnp.bfloat16),
    )


def dotted(first, second):
    return jnp.dot(first, second, preferred_element_type=jnp.float32)


def product(left, right):
    upper = dotted(left[0], right[0])
    lower = dotted(left[1], right[1])
    middle = dotted(left[2], right[2]) - upper - lower
    return balanced(balanced(upper) * SQUARE + balanced(middle) * BASE + lower)


def canonical(values):
    rest = values - jnp.floor(values * INVERSE_MODULUS) * MODULUS
    rest = jnp.where(rest < 0, rest + MODULUS, rest)
    return jnp.where(rest >= MODULUS, rest - MODULUS, rest)


def factor_kernel(
    geometry, ic_rows, places, slots, mask, *refs
):
    piece_count, list_count, run_count = geometry
    pieces = refs[:piece_count]
    lists = refs[piece_count : piece_count + list_count]
    runs = refs[piece_count + list_count : piece_count + list_count + run_count]
    square, left, kept, rows_f32 = refs[piece_count + list_count + run_count :]
    shifts, _, own, width = pieces[0].shape
    size = square.shape[2]
    listed_rows = lists[0].shape[1]
    half = size // 2
    per_place = piece_count // 2

    for number, piece in enumerate(pieces):
        column = pl.multiple_of(places[number // 2] * width, width)
        side = number % 2

        @pl.loop(0, shifts * 2 * BLOCKS)
        def _(step, piece=piece, column=column, side=side):
            shift = step // (2 * BLOCKS)
            matrix = step % (2 * BLOCKS)
            row = pl.multiple_of(ic_rows[side * shifts + shift] * own, own)
            parts = digits(centred(piece[shift, matrix]))
            for limb in range(3):
                square[limb, matrix, pl.ds(row, own), pl.ds(column, width)] = parts[limb]

    tile_rows = listed_rows // (mask.shape[0] // BLOCKS)
    for number, piece in enumerate(lists):
        column = pl.multiple_of(places[number] * width, width)
        for block in range(BLOCKS):
            for tile in range(listed_rows // tile_rows):
                keep = mask[block * (listed_rows // tile_rows) + tile].astype(jnp.float32)
                span = pl.ds(tile * tile_rows, tile_rows)
                rows_f32[block, span, pl.ds(column, width)] = (
                    centred(piece[block, span, :]) * keep
                )

    own_row = pl.multiple_of(slots[0] * own, own)

    def spread(target, rows, values, columns):
        parts = digits(values)
        for limb in range(3):
            target[limb, pl.ds(0, rows), columns] = parts[limb]

    def times(source, rows, matrix, columns, depth):
        return product(
            [source[limb, pl.ds(0, rows), pl.ds(0, depth)] for limb in range(3)],
            [square[limb, matrix, pl.ds(0, depth), columns] for limb in range(3)],
        )

    column_tiles = (pl.ds(0, half), pl.ds(half, half))
    pair_slot = {(0, 1): 0, (0, 2): 1, (1, 2): 2}
    for block in range(BLOCKS):
        rows = listed_rows + block * own
        for columns in column_tiles:
            if block == 0:
                pending = rows_f32[0, pl.ds(0, rows), columns]
            else:
                coupled = None
                for earlier in range(block):
                    height = listed_rows + (earlier + 1) * own
                    term = times(
                        kept.at[earlier], height, pair_slot[earlier, block], columns, size
                    )
                    if height < rows:
                        term = jnp.concatenate(
                            [term, jnp.zeros((rows - height, half), jnp.float32)], axis=0
                        )
                    coupled = term if coupled is None else coupled + term
                listed = jnp.concatenate(
                    [
                        rows_f32[block, pl.ds(0, listed_rows), columns],
                        jnp.zeros((rows - listed_rows, half), jnp.float32),
                    ],
                    axis=0,
                )
                pending = balanced(listed - coupled)
            spread(left, rows, pending, columns)
        for number, columns in enumerate(column_tiles):
            depth = half if number == 0 else size
            solved = times(left, rows, BLOCKS + block, columns, depth)
            rows_f32[block, pl.ds(0, rows), columns] = solved
            own_part = (
                square[0, BLOCKS + block, pl.ds(own_row, own), columns].astype(jnp.float32)
                * BASE
                + square[1, BLOCKS + block, pl.ds(own_row, own), columns].astype(jnp.float32)
            )
            rows_f32[block, pl.ds(rows, own), columns] = own_part
            if block + 1 < BLOCKS:
                spread(
                    kept.at[block], rows + own, jnp.concatenate([solved, own_part], axis=0), columns
                )
        below = rows_f32.shape[1] - rows - own
        if below:
            rows_f32[block, pl.ds(rows + own, below), :] = jnp.zeros((below, size), jnp.float32)

    total = rows_f32.shape[1]
    lane = lax.broadcasted_iota(jnp.int32, (total, LANES), 1)

    def fetch(block, slot, upper):
        source = slots[slot]
        values = rows_f32[
            block, :, pl.ds(pl.multiple_of((source // 2) * LANES, LANES), LANES)
        ]
        odd = source % 2 == 1
        turned = pltpu.roll(values, LANES // 2, 1)
        return jnp.where(odd != upper, turned, values)

    def paired(first, second):
        return jnp.where(lane < LANES // 2, fetch(*first, False), fetch(*second, True))

    def write(run, start, values, count):
        parts = digits(values)
        for limb in range(3):
            runs[run][limb, :, pl.ds(start, count)] = parts[limb][:, :count]

    for run in range(run_count):
        if run in (0, run_count - 1):
            slot = 0 if run == 0 else slots.shape[0] - 1
            write(run, 0, paired((0, slot), (1, slot)), LANES)
            write(run, LANES, fetch(2, slot, False), LANES // 2)
        else:
            for block in range(BLOCKS):
                write(
                    run,
                    block * LANES,
                    paired((block, 2 * run - 1), (block, 2 * run)),
                    LANES,
                )


def left_factor(ic_rows, places, slots, mask, pieces, lists):
    own = pieces[0].shape[2]
    listed_rows = lists[0].shape[1]
    size = pieces[0].shape[3] * len(lists)
    total = listed_rows + BLOCKS * own
    run_count = slots.shape[0] // 2 + 1
    shapes = [
        jax.ShapeDtypeStruct(
            (3, total, BLOCKS * own * (1 if run in (0, run_count - 1) else 2)), jnp.bfloat16
        )
        for run in range(run_count)
    ]
    whole = pl.BlockSpec(memory_space=pltpu.VMEM)
    return pl.pallas_call(
        functools.partial(factor_kernel, (len(pieces), len(lists), run_count)),
        out_shape=shapes,
        in_specs=[pl.BlockSpec(memory_space=pltpu.SMEM)] * 4
        + [whole] * (len(pieces) + len(lists)),
        out_specs=[whole] * run_count,
        scratch_shapes=[
            pltpu.VMEM((3, 2 * BLOCKS, size, size), jnp.bfloat16),
            pltpu.VMEM((3, total, size), jnp.bfloat16),
            pltpu.VMEM((BLOCKS - 1, 3, total, size), jnp.bfloat16),
            pltpu.VMEM((BLOCKS, total, size), jnp.float32),
        ],
        cost_estimate=pl.CostEstimate(
            flops=2 * 3 * 6 * total * size * size,
            bytes_accessed=4 * 6 * size * size,
            transcendentals=0,
        ),
        name="left_factor",
    )(ic_rows, places, slots, mask, *pieces, *lists)


def product_kernel(layout, *refs):
    run_sides, with_total, finish, own = layout
    number = 0
    sides = []
    for counts in run_sides:
        group = []
        for count in counts:
            group.append(refs[number : number + count])
            number += count
        sides.append(group)
    factors = refs[number : number + len(run_sides)]
    number += len(run_sides)
    total_ref = None
    if with_total:
        total_ref = refs[number]
        number += 1
    if finish:
        rest_in = refs[number]
        number += 1
        pivots_out, rest_out = refs[number : number + 2]
        number += 2
    else:
        total_out = refs[number]
        number += 1
    stage = refs[number]
    half = pl.program_id(0)

    def load(group, limit):
        for side in range(2):
            chosen = [arrays[min(side, len(arrays) - 1)] for arrays in group]
            if all(len(arrays) == 1 for arrays in group) and side == 1:
                continue

            def place(chosen=chosen):
                parts = []
                for block in range(BLOCKS):
                    for array in chosen:
                        parts.append(array[block])
                values = digits(centred(jnp.concatenate(parts, axis=0)))
                for limb in range(3):
                    stage[limb, pl.ds(0, limit), :] = values[limb]

            if all(len(arrays) == 1 for arrays in group):
                place()
            else:
                pl.when(half == side)(place)

    summed = None
    for group, factor in zip(sides, factors):
        depth = factor.shape[2]
        load(group, depth)
        term = product(
            [factor[limb] for limb in range(3)],
            [stage[limb, pl.ds(0, depth), :] for limb in range(3)],
        )
        summed = term if summed is None else summed + term
    if with_total:
        summed = summed + total_ref[...]
    if not finish:
        total_out[...] = summed
        return
    listed_rows = rest_in.shape[0]
    rest_out[...] = canonical(rest_in[...] - summed[:listed_rows]) * INVERSE_MODULUS
    solved = canonical(summed[listed_rows:]) * INVERSE_MODULUS
    for block in range(BLOCKS):
        pivots_out[block] = solved[block * own : (block + 1) * own]


def large_product(groups, factors, total, rest, columns, own, name):
    tile = 256
    per_half = columns // 2 // tile
    rows = factors[0].shape[1]

    def spec_for(arrays, side):
        if len(arrays) == 1:
            return pl.BlockSpec((BLOCKS, own, tile), lambda h, j: (0, 0, h * per_half + j))
        if side == 0:
            return pl.BlockSpec(
                (BLOCKS, own, tile), lambda h, j: (0, 0, jnp.where(h == 0, j, per_half - 1))
            )
        return pl.BlockSpec((BLOCKS, own, tile), lambda h, j: (0, 0, jnp.where(h == 0, 0, j)))

    operands, specs, run_sides = [], [], []
    for group in groups:
        counts = []
        for arrays in group:
            counts.append(len(arrays))
            for side, array in enumerate(arrays):
                operands.append(array)
                specs.append(spec_for(arrays, side))
        run_sides.append(tuple(counts))
    for factor in factors:
        operands.append(factor)
        specs.append(pl.BlockSpec(factor.shape, lambda h, j: (0, 0, 0)))
    wide = pl.BlockSpec((rows, tile), lambda h, j: (0, h * per_half + j))
    if total is not None:
        operands.append(total)
        specs.append(wide)
    finish = rest is not None
    if finish:
        listed = pl.BlockSpec((rest.shape[0], tile), lambda h, j: (0, h * per_half + j))
        operands.append(rest)
        specs.append(listed)
        shapes = [
            jax.ShapeDtypeStruct((BLOCKS, own, columns), jnp.float32),
            jax.ShapeDtypeStruct(rest.shape, jnp.float32),
        ]
        outs = [pl.BlockSpec((BLOCKS, own, tile), lambda h, j: (0, 0, h * per_half + j)), listed]
    else:
        shapes = jax.ShapeDtypeStruct((rows, columns), jnp.float32)
        outs = wide
    depth = max(factor.shape[2] for factor in factors)
    depths = sum(factor.shape[2] for factor in factors)
    return pl.pallas_call(
        functools.partial(
            product_kernel, (tuple(run_sides), total is not None, finish, own)
        ),
        grid=(2, per_half),
        in_specs=specs,
        out_specs=outs,
        out_shape=shapes,
        scratch_shapes=[pltpu.VMEM((3, depth, tile), jnp.bfloat16)],
        cost_estimate=pl.CostEstimate(
            flops=2 * 3 * rows * depths * columns,
            bytes_accessed=4 * columns * (depths + 2 * rows),
            transcendentals=0,
        ),
        name=name,
    )(*operands)


def ring_body(row_count, col_count, pivot_rows, coupling, inverse, multipliers, tile_mask, rest):
    own, columns = pivot_rows.shape[1:]
    levels = row_count // 2
    half = columns // 2
    row = lax.axis_index("row")
    col = lax.axis_index("col")

    def row_at(place):
        place = place % row_count
        return 2 * place if place < levels else 2 * (2 * levels - 1 - place) + 1

    forward = [(row_at(p), row_at(p + 1)) for p in range(row_count)]
    backward = [(b, a) for a, b in forward]
    side_swap = [(r, r ^ 1) for r in range(row_count)]

    def level_shift(k):
        return [(r, ((r // 2 + k) % levels) * 2 + r % 2) for r in range(row_count)]

    def col_swap(bit):
        return [(c, c ^ bit) for c in range(col_count)]

    square = jnp.concatenate([coupling, inverse], axis=0)
    shifted = [square] + [lax.ppermute(square, "row", level_shift(k)) for k in range(1, levels)]
    near = jnp.stack(shifted)
    far = lax.ppermute(near, "row", side_swap)
    pieces = [[near, far]]
    lists = [multipliers]
    rel = [0]
    bit = col_count // 2
    while bit:
        pieces = pieces + [[lax.ppermute(a, "col", col_swap(bit)) for a in pair] for pair in pieces]
        lists = lists + [lax.ppermute(a, "col", col_swap(bit)) for a in lists]
        rel = rel + [r ^ bit for r in rel]
        bit //= 2

    starts = [pivot_rows[:, :, :half], pivot_rows[:, :, half:]]
    ahead = [starts]
    back = [starts]
    for step in range(1, levels):
        ahead.append([lax.ppermute(a, "row", forward) for a in ahead[-1]])
        back.append([lax.ppermute(a, "row", backward) for a in back[-1]])
    last = [
        lax.ppermute(ahead[-1][0], "row", forward),
        lax.ppermute(back[-1][1], "row", backward),
    ]

    place = jnp.where(row % 2 == 0, row // 2, 2 * levels - 1 - row // 2)
    offsets = [0]
    for step in range(1, levels):
        offsets += [-step, step]
    offsets.append(levels)
    spots = (place + jnp.array(offsets, jnp.int32) + row_count) % row_count
    slots = jnp.where(spots < levels, 2 * spots, 2 * (2 * levels - 1 - spots) + 1).astype(jnp.int32)
    ks = jnp.arange(levels, dtype=jnp.int32)
    level_rows = ((row // 2 - ks + levels) % levels) * 2
    ic_rows = jnp.concatenate([level_rows + row % 2, level_rows + (1 - row % 2)]).astype(jnp.int32)
    places = (col ^ jnp.array(rel, jnp.int32)).astype(jnp.int32)

    factors = left_factor(
        ic_rows,
        places,
        slots,
        tile_mask.reshape(-1),
        [a for pair in pieces for a in pair],
        lists,
    )
    total = large_product(
        [[[pivot_rows]]] + [[ahead[s], back[s]] for s in range(1, levels - 1)],
        factors[: levels - 1],
        None,
        None,
        columns,
        own,
        "product_early",
    )
    total = large_product(
        [[ahead[levels - 1], back[levels - 1]]],
        factors[levels - 1 : levels],
        total,
        None,
        columns,
        own,
        "product_late",
    )
    return large_product(
        [[last]], factors[levels:], total, rest, columns, own, "product_last"
    )


def reduce_mod(values):
    quotient = jnp.floor(values / MODULUS)
    rest = values - quotient * MODULUS
    rest = jnp.where(rest < 0, rest + MODULUS, rest)
    return jnp.where(rest >= MODULUS, rest - MODULUS, rest)


def product_mod(left, right):
    summed = None
    for first in range(0, left.shape[1], 512):
        last = min(first + 512, left.shape[1])
        portion = product(
            digits(centred(left[:, first:last])), digits(centred(right[first:last]))
        )
        summed = portion if summed is None else summed + portion
    return reduce_mod(summed)


def plain_body(pivot_rows, coupling, inverse, multipliers, tile_mask, nonpivot_rows):
    coupling_rows, inverse_rows = (
        lax.all_gather(coupling, "col", axis=2, tiled=True),
        lax.all_gather(inverse, "col", axis=2, tiled=True),
    )
    solve_left = lax.all_gather(inverse_rows, "row", axis=1, tiled=True)
    own_count = pivot_rows.shape[1]
    listed = multipliers * jnp.repeat(
        tile_mask.astype(jnp.float32), multipliers.shape[1] // tile_mask.shape[1], axis=1
    )[:, :, None]
    pair_slot = {(0, 1): 0, (0, 2): 1, (1, 2): 2}
    whole = [None] * BLOCKS
    own_blocks = [None] * BLOCKS
    update = jnp.zeros(nonpivot_rows.shape, jnp.float32)
    for block in reversed(range(BLOCKS)):
        pending = pivot_rows[block]
        for later in range(block + 1, BLOCKS):
            pending = pending - product_mod(coupling_rows[pair_slot[block, later]], whole[later])
        pending = reduce_mod(pending)
        whole[block] = product_mod(
            solve_left[block], lax.all_gather(pending, "row", axis=0, tiled=True)
        )
        own_blocks[block] = lax.dynamic_slice_in_dim(
            whole[block], lax.axis_index("row") * own_count, own_count, 0
        )
        update = update + product_mod(
            lax.all_gather(listed[block], "col", axis=1, tiled=True), whole[block]
        )
    residue = reduce_mod(nonpivot_rows - update)
    return jnp.stack(own_blocks) / MODULUS, residue / MODULUS


def body(row_count, col_count, pivot_rows, coupling, inverse, multipliers, tile_mask, rest):
    own, columns = pivot_rows.shape[1:]
    fits = (
        own * 2 == LANES
        and coupling.shape[2] % LANES == 0
        and own * row_count <= 512
        and row_count % 2 == 0
        and row_count >= 6
        and col_count & (col_count - 1) == 0
        and columns % 512 == 0
    )
    args = (pivot_rows, coupling, inverse, multipliers, tile_mask, rest)
    if fits:
        return ring_body(row_count, col_count, *args)
    return plain_body(*args)


def solution(mesh):
    in_specs = (
        P(None, "row", "col"),
        P(None, "row", "col"),
        P(None, "row", "col"),
        P(None, "row", "col"),
        P(None, "row"),
        P("row", "col"),
    )
    out_specs = (P(None, "row", "col"), P("row", "col"))
    return jax.shard_map(
        functools.partial(body, mesh.shape["row"], mesh.shape["col"]),
        mesh=mesh,
        in_specs=in_specs,
        out_specs=out_specs,
        check_vma=False,
    )
```

```python
import functools

import jax
import jax.numpy as jnp
from jax import lax
from jax.experimental import pallas as pl
from jax.experimental.pallas import tpu as pltpu
from jax.sharding import PartitionSpec as P


MODULUS = 32003.0
INVERSE_MODULUS = 1.0 / 32003.0
HALF = 16001.0
BASE = 179.0
INVERSE_BASE = 1.0 / 179.0
FACTOR_VMEM = 36 * 2**20
PRODUCT_VMEM = 20 * 2**20
BLOCKS = 3
LANES = 128


def balanced(values):
    return values - jnp.round(values * INVERSE_MODULUS) * MODULUS


def centred(values):
    return jnp.where(values > HALF, values - MODULUS, values)


def digits(values):
    upper = jnp.round(values * INVERSE_BASE)
    lower = values - upper * BASE
    return upper.astype(jnp.bfloat16), lower.astype(jnp.bfloat16)


def left_digits(values):
    shifted = digits(balanced(values * BASE))
    plain = digits(values)
    return shifted, plain


def dotted(first, second):
    return jnp.dot(first, second, preferred_element_type=jnp.float32)


def product(left, right):
    shifted, plain = left
    upper = dotted(shifted[0], right[0]) + dotted(plain[0], right[1])
    lower = dotted(shifted[1], right[0]) + dotted(plain[1], right[1])
    return balanced(balanced(upper) * BASE + lower)


def factor_kernel(geometry, ic_rows, places, slots, mask, *refs):
    piece_count, list_count, run_slots = geometry
    run_count = len(run_slots)
    pieces = refs[:piece_count]
    lists = refs[piece_count : piece_count + list_count]
    runs = refs[piece_count + list_count : piece_count + list_count + run_count]
    square, left, kept, rows_f32 = refs[piece_count + list_count + run_count :]
    shifts, _, own, width = pieces[0].shape
    size = square.shape[2]
    listed_rows = lists[0].shape[1]
    half = size // 2

    for number, piece in enumerate(pieces):
        column = pl.multiple_of(places[number // 2] * width, width)
        side = number % 2

        @pl.loop(0, shifts * 2 * BLOCKS)
        def _(step, piece=piece, column=column, side=side):
            shift = step // (2 * BLOCKS)
            matrix = step % (2 * BLOCKS)
            row = ic_rows[side * shifts + shift] * own
            first = pl.multiple_of(row + (row // half) * half, own)
            upper, lower = digits(piece[shift, matrix])
            square[matrix, pl.ds(first, own), pl.ds(column, width)] = upper
            square[matrix, pl.ds(first + half, own), pl.ds(column, width)] = lower

    tiles = mask.shape[0] // BLOCKS
    tile_rows = listed_rows // tiles
    for number, piece in enumerate(lists):
        column = pl.multiple_of(places[number] * width, width)
        for block in range(BLOCKS):
            for tile in range(tiles):
                keep = -mask[block * tiles + tile].astype(jnp.float32)
                span = pl.ds(tile * tile_rows, tile_rows)
                rows_f32[block, span, pl.ds(column, width)] = (
                    centred(piece[block, span, :]) * keep
                )

    own_first = slots[0] * own
    own_first = pl.multiple_of(own_first + (own_first // half) * half, own)

    def spread(target, rows, values, number):
        for part, pair in enumerate(left_digits(values)):
            columns = pl.ds(number * size + part * half, half)
            target[0, pl.ds(0, rows), columns] = pair[0]
            target[1, pl.ds(0, rows), columns] = pair[1]

    def times(source, rows, matrix, columns, depth):
        right = square[matrix, pl.ds(0, depth), columns]
        upper = dotted(source[0, pl.ds(0, rows), pl.ds(0, depth)], right)
        lower = dotted(source[1, pl.ds(0, rows), pl.ds(0, depth)], right)
        return balanced(balanced(upper) * BASE + lower)

    column_tiles = (pl.ds(0, half), pl.ds(half, half))
    pair_slot = {(0, 1): 0, (0, 2): 1, (1, 2): 2}
    for block in range(BLOCKS):
        rows = listed_rows + block * own
        for number, columns in enumerate(column_tiles):
            if block == 0:
                pending = rows_f32[0, pl.ds(0, rows), columns]
            else:
                coupled = None
                for earlier in range(block):
                    height = listed_rows + (earlier + 1) * own
                    term = times(
                        kept.at[earlier], height, pair_slot[earlier, block], columns, 2 * size
                    )
                    if height < rows:
                        term = jnp.concatenate(
                            [term, jnp.zeros((rows - height, half), jnp.float32)], axis=0
                        )
                    coupled = term if coupled is None else coupled + term
                listed = jnp.concatenate(
                    [
                        rows_f32[block, pl.ds(0, listed_rows), columns],
                        jnp.zeros((rows - listed_rows, half), jnp.float32),
                    ],
                    axis=0,
                )
                pending = balanced(listed - coupled)
            spread(left, rows, pending, number)
        for number, columns in enumerate(column_tiles):
            depth = size if number == 0 else 2 * size
            solved = times(left, rows, BLOCKS + block, columns, depth)
            rows_f32[block, pl.ds(0, rows), columns] = solved
            matrix = BLOCKS + block
            upper = square[matrix, pl.ds(own_first, own), columns].astype(jnp.float32)
            lower = square[matrix, pl.ds(own_first + half, own), columns].astype(jnp.float32)
            own_part = centred(upper * BASE + lower)
            rows_f32[block, pl.ds(rows, own), columns] = own_part
            if block + 1 < BLOCKS:
                whole = jnp.concatenate([solved, own_part], axis=0)
                spread(kept.at[block], rows + own, whole, number)
        below = rows_f32.shape[1] - rows - own
        if below:
            rows_f32[block, pl.ds(rows + own, below), :] = jnp.zeros((below, size), jnp.float32)

    total = rows_f32.shape[1]
    lane = lax.broadcasted_iota(jnp.int32, (total, LANES), 1)

    def fetch(slot, block, upper):
        source = slots[slot]
        first = pl.multiple_of((source // 2) * LANES, LANES)
        values = rows_f32[block, :, pl.ds(first, LANES)]
        odd = source % 2 == 1
        return jnp.where(odd != upper, pltpu.roll(values, LANES // 2, 1), values)

    for run, chosen in zip(runs, run_slots):
        segments = [(s, b) for s in chosen for b in range(BLOCKS)]
        count = len(segments)
        line = [(True, s) for s in segments] + [(False, s) for s in segments]
        for number in range(count):
            (first_part, first), (second_part, second) = line[2 * number : 2 * number + 2]
            low, high = fetch(*first, False), fetch(*second, True)
            if first_part and not second_part:
                low = balanced(low * BASE)
            values = jnp.where(lane < LANES // 2, low, high)
            if second_part:
                values = balanced(values * BASE)
            parts = digits(values)
            for limb in range(2):
                run[limb, :, pl.ds(number * LANES, LANES)] = parts[limb]


def left_factor(ic_rows, places, slots, mask, pieces, lists, run_slots):
    own = pieces[0].shape[2]
    listed_rows = lists[0].shape[1]
    size = pieces[0].shape[3] * len(lists)
    total = listed_rows + BLOCKS * own
    shapes = [
        jax.ShapeDtypeStruct((2, total, 2 * BLOCKS * own * len(chosen)), jnp.bfloat16)
        for chosen in run_slots
    ]
    whole = pl.BlockSpec(memory_space=pltpu.VMEM)
    return pl.pallas_call(
        functools.partial(factor_kernel, (len(pieces), len(lists), run_slots)),
        out_shape=shapes,
        in_specs=[pl.BlockSpec(memory_space=pltpu.SMEM)] * 4
        + [whole] * (len(pieces) + len(lists)),
        out_specs=[whole] * len(shapes),
        scratch_shapes=[
            pltpu.VMEM((2 * BLOCKS, 2 * size, size), jnp.bfloat16),
            pltpu.VMEM((2, total, 2 * size), jnp.bfloat16),
            pltpu.VMEM((BLOCKS - 1, 2, total, 2 * size), jnp.bfloat16),
            pltpu.VMEM((BLOCKS, total, size), jnp.float32),
        ],
        cost_estimate=pl.CostEstimate(
            flops=2 * 4 * 6 * total * size * size,
            bytes_accessed=4 * 6 * size * size,
            transcendentals=0,
        ),
        compiler_params=pltpu.CompilerParams(vmem_limit_bytes=FACTOR_VMEM),
        name="left_factor",
    )(ic_rows, places, slots, mask, *pieces, *lists)


def product_kernel(layout, *refs):
    piece_sides, tight, base_kind, finish, own = layout
    number = 0
    runs = []
    for counts in piece_sides:
        group = []
        for count in counts:
            group.append(refs[number : number + count])
            number += count
        runs.append(group)
    factors = refs[number : number + len(runs)]
    number += len(runs)
    base = refs[number]
    number += 1
    if finish:
        number += finish - 1
        pivots_out, rest_out = refs[number : number + 2]
        number += 2
    else:
        total_out = refs[number]
        number += 1
    stage = refs[number]

    def place(pieces, side, depth):
        first = 0
        for arrays in pieces:
            array = arrays[min(side, len(arrays) - 1)]
            for block in range(BLOCKS):
                values = array[block]
                count = values.shape[0]
                upper, lower = digits(centred(values) if tight else values)
                row = first + block * own
                stage[pl.ds(row, count), :] = upper
                stage[pl.ds(depth + row, count), :] = lower
            first += count if (first + count) % own else BLOCKS * own + count - own

    upper = lower = None
    for pieces, factor in zip(runs, factors):
        depth = factor.shape[2] // 2
        if any(len(arrays) > 1 for arrays in pieces):
            for side in range(2):
                pl.when(pl.program_id(0) == side)(
                    functools.partial(place, pieces, side, depth)
                )
        else:
            place(pieces, 0, depth)
        right = stage[pl.ds(0, 2 * depth), :]
        here = dotted(factor[0], right)
        upper = here if upper is None else upper + here
        here = dotted(factor[1], right)
        lower = here if lower is None else lower + here
    summed = balanced(upper) * BASE + (balanced(lower) if tight else lower)
    if not finish:
        summed = balanced(summed)
        if base_kind == "rest":
            listed_rows = base.shape[0]
            total_out[pl.ds(0, listed_rows), :] = summed[:listed_rows] + base[...]
            own_rows = summed.shape[0] - listed_rows
            total_out[pl.ds(listed_rows, own_rows), :] = summed[listed_rows:]
        else:
            total_out[...] = summed + base[...]
        return
    summed = balanced(summed + base[...])
    summed = jnp.where(summed < 0, summed + MODULUS, summed) * INVERSE_MODULUS
    listed_rows = rest_out.shape[0]
    rest_out[...] = summed[:listed_rows]
    for block in range(BLOCKS):
        first = listed_rows + block * own
        pivots_out[block] = summed[first : first + own]


def large_product(runs, factors, base, base_kind, span, columns, own, rest_rows, outs):
    tile = 256
    per_half = columns // 2 // tile
    first_half, half_count = span
    rows = factors[0].shape[1]

    def column(h, j):
        return (first_half + h) * per_half + j

    operands, specs, sides = [], [], []
    for pieces in runs:
        counts = []
        for arrays in pieces:
            counts.append(len(arrays))
            for side, array in enumerate(arrays):
                operands.append(array)
                if array.shape[2] == columns:
                    index = lambda h, j: (0, 0, column(h, j))
                elif len(arrays) == 1:
                    index = lambda h, j: (0, 0, j)
                elif side == 0:
                    index = lambda h, j: (0, 0, jnp.where(h == 0, j, per_half - 1))
                else:
                    index = lambda h, j: (0, 0, jnp.where(h == 0, 0, j))
                specs.append(pl.BlockSpec((BLOCKS, array.shape[1], tile), index))
        sides.append(tuple(counts))
    for factor in factors:
        operands.append(factor)
        specs.append(pl.BlockSpec(factor.shape, lambda h, j: (0, 0, 0)))
    operands.append(base)
    if base.shape[1] == columns:
        specs.append(pl.BlockSpec((base.shape[0], tile), lambda h, j: (0, column(h, j))))
    else:
        specs.append(pl.BlockSpec((base.shape[0], tile), lambda h, j: (0, j)))
    aliases = {}
    finish = 0
    if outs == "total":
        shapes = jax.ShapeDtypeStruct((rows, columns * half_count // 2), jnp.float32)
        out_specs = pl.BlockSpec((rows, tile), lambda h, j: (0, h * per_half + j))
    else:
        finish = 1
        shapes = [
            jax.ShapeDtypeStruct((BLOCKS, own, columns), jnp.float32),
            jax.ShapeDtypeStruct((rest_rows, columns), jnp.float32),
        ]
        out_specs = [
            pl.BlockSpec((BLOCKS, own, tile), lambda h, j: (0, 0, column(h, j))),
            pl.BlockSpec((rest_rows, tile), lambda h, j: (0, column(h, j))),
        ]
        for number, array in enumerate(outs):
            aliases[len(operands)] = number
            operands.append(array)
            specs.append(pl.BlockSpec(memory_space=pl.ANY))
            finish += 1
    depths = sum(factor.shape[2] for factor in factors)
    tight = depths // 2 > 576
    deepest = max(factor.shape[2] for factor in factors)
    return pl.pallas_call(
        functools.partial(product_kernel, (tuple(sides), tight, base_kind, finish, own)),
        grid=(half_count, per_half),
        in_specs=specs,
        out_specs=out_specs,
        out_shape=shapes,
        input_output_aliases=aliases,
        scratch_shapes=[pltpu.VMEM((deepest, tile), jnp.bfloat16)],
        cost_estimate=pl.CostEstimate(
            flops=2 * 2 * rows * depths * columns * half_count // 2,
            bytes_accessed=4 * columns * (depths // 2 + 2 * rows) * half_count // 2,
            transcendentals=0,
        ),
        compiler_params=pltpu.CompilerParams(vmem_limit_bytes=PRODUCT_VMEM),
    )(*operands)


def ring_program(row_count, col_count, pivot_rows, coupling, inverse, multipliers, tile_mask, rest):
    own, columns = pivot_rows.shape[1:]
    levels = row_count // 2
    half = columns // 2
    row = lax.axis_index("row")
    col = lax.axis_index("col")

    def row_at(place):
        place = place % row_count
        return 2 * place if place < levels else 2 * (2 * levels - 1 - place) + 1

    forward = [(row_at(p), row_at(p + 1)) for p in range(row_count)]
    backward = [(b, a) for a, b in forward]
    side_swap = [(r, r ^ 1) for r in range(row_count)]

    def level_shift(k):
        return [(r, ((r // 2 + k) % levels) * 2 + r % 2) for r in range(row_count)]

    def col_swap(bit):
        return [(c, c ^ bit) for c in range(col_count)]

    square = jnp.concatenate([coupling, inverse], axis=0)
    shifted = [lax.ppermute(square, "row", level_shift(k)) for k in range(1, levels)]
    near = jnp.stack([square] + shifted)
    far = lax.ppermute(near, "row", side_swap)
    pieces = [[near, far]]
    lists = [multipliers]
    rel = [0]
    bit = col_count // 2
    while bit:
        pieces = pieces + [
            [
                lax.ppermute(near_piece, "col", col_swap(bit)),
                lax.ppermute(far_piece, "col", col_swap(bit)),
            ]
            for near_piece, far_piece in pieces
        ]
        lists = lists + [lax.ppermute(a, "col", col_swap(bit)) for a in lists]
        rel = rel + [r ^ bit for r in rel]
        bit //= 2

    starts = [pivot_rows[:, :, :half], pivot_rows[:, :, half:]]
    ahead = [starts]
    back = [starts]
    for _ in range(1, levels):
        ahead.append([lax.ppermute(a, "row", forward) for a in ahead[-1]])
        back.append([lax.ppermute(a, "row", backward) for a in back[-1]])
    middle = own // 2
    last = []
    for n in range(2):
        first = lax.ppermute(ahead[-1][n][:, :middle], "row", forward)
        second = lax.ppermute(back[-1][n][:, middle:], "row", backward)
        last.append([[first], [second]])

    place = jnp.where(row % 2 == 0, row // 2, 2 * levels - 1 - row // 2)
    offsets = [0]
    for step in range(1, levels):
        offsets += [-step, step]
    offsets.append(levels)
    spots = (place + jnp.array(offsets, jnp.int32) + row_count) % row_count
    slots = jnp.where(spots < levels, 2 * spots, 2 * (2 * levels - 1 - spots) + 1).astype(jnp.int32)
    ks = jnp.arange(levels, dtype=jnp.int32)
    level_rows = ((row // 2 - ks + levels) % levels) * 2
    ic_rows = jnp.concatenate([level_rows + row % 2, level_rows + (1 - row % 2)]).astype(jnp.int32)
    places = (col ^ jnp.array(rel, jnp.int32)).astype(jnp.int32)

    early_slots = tuple(range(2 * levels - 3))
    late_slots = (2 * levels - 3, 2 * levels - 2)
    early_factor, late_factor, last_factor = left_factor(
        ic_rows,
        places,
        slots,
        tile_mask.reshape(-1),
        [a for pair in pieces for a in pair],
        lists,
        (early_slots, late_slots, (2 * levels - 1,)),
    )
    sizes = (columns, own, rest.shape[0])
    early_pieces = [[pivot_rows]]
    for step in range(1, levels - 1):
        early_pieces += [ahead[step], back[step]]
    total = large_product([early_pieces], [early_factor], rest, "rest", (0, 2), *sizes, "total")
    pairs = [[[ahead[-1][n]], [back[-1][n]]] for n in range(2)]
    outs = large_product(
        [pairs[0], last[0]], [late_factor, last_factor], total, "total", (0, 1), *sizes, ()
    )
    total = large_product([pairs[1]], [late_factor], total, "total", (1, 1), *sizes, "total")
    return large_product([last[1]], [last_factor], total, "total", (1, 1), *sizes, tuple(outs))


def reduce_mod(values):
    quotient = jnp.floor(values / MODULUS)
    rest = values - quotient * MODULUS
    rest = jnp.where(rest < 0, rest + MODULUS, rest)
    return jnp.where(rest >= MODULUS, rest - MODULUS, rest)


def product_mod(left, right):
    summed = None
    for first in range(0, left.shape[1], 512):
        last = min(first + 512, left.shape[1])
        portion = product(left_digits(centred(left[:, first:last])), digits(right[first:last]))
        summed = portion if summed is None else summed + portion
    return reduce_mod(summed)


def plain_body(pivot_rows, coupling, inverse, multipliers, tile_mask, nonpivot_rows):
    coupling_rows, inverse_rows = (
        lax.all_gather(coupling, "col", axis=2, tiled=True),
        lax.all_gather(inverse, "col", axis=2, tiled=True),
    )
    solve_left = lax.all_gather(inverse_rows, "row", axis=1, tiled=True)
    own_count = pivot_rows.shape[1]
    listed = multipliers * jnp.repeat(
        tile_mask.astype(jnp.float32), multipliers.shape[1] // tile_mask.shape[1], axis=1
    )[:, :, None]
    pair_slot = {(0, 1): 0, (0, 2): 1, (1, 2): 2}
    whole = [None] * BLOCKS
    own_blocks = [None] * BLOCKS
    update = jnp.zeros(nonpivot_rows.shape, jnp.float32)
    for block in reversed(range(BLOCKS)):
        pending = pivot_rows[block]
        for later in range(block + 1, BLOCKS):
            pending = pending - product_mod(coupling_rows[pair_slot[block, later]], whole[later])
        pending = reduce_mod(pending)
        whole[block] = product_mod(
            solve_left[block], lax.all_gather(pending, "row", axis=0, tiled=True)
        )
        own_blocks[block] = lax.dynamic_slice_in_dim(
            whole[block], lax.axis_index("row") * own_count, own_count, 0
        )
        update = update + product_mod(
            lax.all_gather(listed[block], "col", axis=1, tiled=True), whole[block]
        )
    residue = reduce_mod(nonpivot_rows - update)
    return jnp.stack(own_blocks) / MODULUS, residue / MODULUS


def ring_fits(row_count, col_count):
    return row_count == 2 * 4 and col_count >= 2 and col_count & (col_count - 1) == 0


def body(row_count, col_count, pivot_rows, coupling, inverse, multipliers, tile_mask, rest):
    own, columns = pivot_rows.shape[1:]
    fits = (
        ring_fits(row_count, col_count)
        and own * 2 == LANES
        and coupling.shape[2] % LANES == 0
        and columns % 512 == 0
    )
    args = (pivot_rows, coupling, inverse, multipliers, tile_mask, rest)
    if fits:
        return ring_program(row_count, col_count, *args)
    return plain_body(*args)


def solution(mesh):
    in_specs = (
        P(None, "row", "col"),
        P(None, "row", "col"),
        P(None, "row", "col"),
        P(None, "row", "col"),
        P(None, "row"),
        P("row", "col"),
    )
    out_specs = (P(None, "row", "col"), P("row", "col"))
    return jax.shard_map(
        functools.partial(body, mesh.shape["row"], mesh.shape["col"]),
        mesh=mesh,
        in_specs=in_specs,
        out_specs=out_specs,
        check_vma=False,
    )
```
